32 devices in a mesh: fsdp: 4 (over x, core), context: 4 (over z), tensor: 2 (over y).
Axes of the slice: x: 2, y: 2, z: 4, core: 2. Of those that a mesh axis runs over, the one named last changes fastest.
Arguments:
- tokens: bfloat16 [32, 1024, 1024], P('fsdp', 'context'), may hold values from -6 to 6
- segments: int32 [32, 1024], P('fsdp'), may hold values from 0 to 4, as said below
- input_gain: bfloat16 [1024], P('fsdp'), may hold values from 0.25 to 1.75
- middle_gain: bfloat16 [1024], P('fsdp'), may hold values from 0.25 to 1.75
- query_gain: bfloat16 [128], P('fsdp'), may hold values from 0.25 to 1.75
- key_gain: bfloat16 [128], P('fsdp'), may hold values from 0.25 to 1.75
- w_query: bfloat16 [1024, 2048], P('fsdp', 'tensor'), may hold values from -0.1875 to 0.1875
- key_projection_weight: bfloat16 [1024, 1024], P('fsdp', 'tensor'), may hold values from -0.1875 to 0.1875
- value_projection_weight: bfloat16 [1024, 1024], P('fsdp', 'tensor'), may hold values from -0.1875 to 0.1875
- w_out: bfloat16 [2048, 1024], P('tensor', 'fsdp'), may hold values from -1.5 to 1.5
- w_gate: bfloat16 [1024, 3072], P('fsdp', 'tensor'), may hold values from -0.1875 to 0.1875
- w_up: bfloat16 [1024, 3072], P('fsdp', 'tensor'), may hold values from -0.1875 to 0.1875
- w_down: bfloat16 [3072, 1024], P('tensor', 'fsdp'), may hold values from -0.109375 to 0.109375
- cotangent: bfloat16 [32, 1024, 1024], P('fsdp', 'context'), may hold values from -6 to 6
Outputs:
- block_out: bfloat16 [32, 1024, 1024], P('fsdp', 'context')
- grad_tokens: bfloat16 [32, 1024, 1024], P('fsdp', 'context')
- grad_input_gain: float32 [1024], P('fsdp')
- grad_middle_gain: float32 [1024], P('fsdp')
- grad_query_gain: float32 [128], P('fsdp')
- grad_key_gain: float32 [128], P('fsdp')
- grad_w_query: float32 [1024, 2048], P('fsdp', 'tensor')
- grad_w_key: float32 [1024, 1024], P('fsdp', 'tensor')
- grad_w_value: float32 [1024, 1024], P('fsdp', 'tensor')
- grad_w_out: float32 [2048, 1024], P('tensor', 'fsdp')
- grad_w_gate: float32 [1024, 3072], P('fsdp', 'tensor')
- grad_w_up: float32 [1024, 3072], P('fsdp', 'tensor')
- grad_w_down: float32 [3072, 1024], P('tensor', 'fsdp')
The draws below stay inside these ranges and needn't reach their ends.
Inputs may be any that keep to these rules, and one draw needn't show every extreme that they name: `segments`: within each sequence the segment numbers start at 0 and never fall. In each aligned block of 8 sequences (those of one index of fsdp) exactly one sequence is a single document, and every other sequence holds exactly five documents.
All inputs are finite; a program needn't handle non-finite values.
Results may differ from the reference program's by a relative error of at most 0.023.
Values may be sent and summed in bfloat16 or wider, within the bound.
No kernel may reach another device: no remote copies, remote signals or barrier semaphores. Data moves between devices by JAX's collectives and lax.ppermute only.
A program may use at most 320 MiB of HBM per device.

```python
import math
import jax
import jax.numpy as jnp
from jax import lax

MODEL_DIMENSION = 1024
QUERY_HEADS = 16
KEY_VALUE_HEADS = 8
HEAD_SIZE = 128
FF = 3072
SEQ_LEN = 1024
SEQS = 8
NSEQ = 32


def draw_segments(key, part):
    cut_key = jax.random.fold_in(key, 11)
    pick_key = jax.random.fold_in(key, 23)
    seq_keys = jax.random.split(cut_key, NSEQ)
    cuts = jax.vmap(lambda one_key: jax.random.permutation(one_key, SEQ_LEN - 1)[:4] + 1)(seq_keys)
    groups = NSEQ // SEQS
    chosen = jax.random.randint(pick_key, (groups,), 0, SEQS)
    seq_index = jnp.arange(NSEQ)
    single = seq_index % SEQS == jnp.repeat(chosen, SEQS)
    places = jnp.arange(SEQ_LEN)
    counts = jnp.sum((places[None, :, None] >= cuts[:, None, :]).astype(jnp.int32), axis=-1)
    return jnp.where(single[:, None], 0, counts).astype(jnp.int32)


def spiked(values, rng, source, target, shards_of, factor):
    owner, partner = [(jnp.arange(values.shape[dim]) // (values.shape[dim] // shards_of)).reshape([-1 if axis == dim else 1 for axis in range(values.ndim)]) for dim in (source, target)]
    chosen = jax.random.permutation(rng, shards_of)[partner]
    strong = (owner == chosen) | (owner == (partner + shards_of // 2) % shards_of)
    return jnp.where(strong, factor * values, values)


def steps_of(own_key, extent, cuts, low, high):
    gain = 1.0
    for position, parts in cuts:
        draws = jax.random.uniform(jax.random.fold_in(jax.random.fold_in(own_key, 6), position), (parts,), jnp.float32, low / len(cuts), high / len(cuts))
        gain = gain * jnp.repeat(jnp.exp(draws), extent[position] // parts).reshape((-1,) + (1,) * (len(extent) - 1 - position))
    return gain


def centred(key, shape, spread, bound, shards=(), held_as=jnp.bfloat16):
    loudness = steps_of(key, shape, shards, -0.22, 0.18) if shards else 1.0
    result = jax.random.normal(key, shape, jnp.float32) * spread * loudness
    return jnp.minimum(jnp.maximum(result, -bound), bound).astype(held_as)


def heavy_noise(stream_key, extent, scale, bound, cuts, heavy, kind=jnp.bfloat16):
    values = scale * jax.random.normal(stream_key, extent, jnp.float32)
    if cuts:
        values = values * steps_of(stream_key, extent, cuts, -0.22, 0.18)
    return jnp.clip(spiked(values, jax.random.fold_in(stream_key, 3), *heavy), -bound, bound).astype(kind)


def setup_inputs(seed: int = 0) -> dict:
    key_of = jax.random.split(jax.random.key(seed), 15)
    return {
        "tokens": centred(key_of[0], (NSEQ, SEQ_LEN, MODEL_DIMENSION), 1.0, 6.0, ((0, 4), (1, 4))),
        "segments": draw_segments(jax.random.fold_in(key_of[14], 71), 0),
        "input_gain": jnp.clip(1.0 + 0.15 * jax.random.normal(key_of[2], (MODEL_DIMENSION,), jnp.float32), 0.25, 1.75).astype(jnp.bfloat16),
        "middle_gain": jnp.clip(1.0 + 0.15 * jax.random.normal(key_of[3], (MODEL_DIMENSION,), jnp.float32), 0.25, 1.75).astype(jnp.bfloat16),
        "query_gain": jnp.clip(1.0 + 0.15 * jax.random.normal(key_of[4], (HEAD_SIZE,), jnp.float32), 0.25, 1.75).astype(jnp.bfloat16),
        "key_gain": jnp.clip(1.0 + 0.15 * jax.random.normal(key_of[5], (HEAD_SIZE,), jnp.float32), 0.25, 1.75).astype(jnp.bfloat16),
        "w_query": centred(key_of[6], (MODEL_DIMENSION, QUERY_HEADS * HEAD_SIZE), MODEL_DIMENSION ** -0.5, 0.1875, ((0, 4), (1, 2))),
        "key_projection_weight": centred(key_of[7], (MODEL_DIMENSION, KEY_VALUE_HEADS * HEAD_SIZE), MODEL_DIMENSION ** -0.5, 0.1875, ((0, 4), (1, 2))),
        "value_projection_weight": centred(key_of[8], (MODEL_DIMENSION, KEY_VALUE_HEADS * HEAD_SIZE), MODEL_DIMENSION ** -0.5, 0.1875, ((0, 4), (1, 2))),
        "w_out": centred(key_of[9], (QUERY_HEADS * HEAD_SIZE, MODEL_DIMENSION), (QUERY_HEADS * HEAD_SIZE // 128) ** -0.5, 1.5, ((0, 2), (1, 4))),
        "w_gate": centred(key_of[10], (MODEL_DIMENSION, FF), MODEL_DIMENSION ** -0.5, 0.1875, ((0, 4), (1, 2))),
        "w_up": centred(key_of[11], (MODEL_DIMENSION, FF), MODEL_DIMENSION ** -0.5, 0.1875, ((0, 4), (1, 2))),
        "w_down": centred(key_of[12], (FF, MODEL_DIMENSION), FF ** -0.5, 0.109375, ((0, 2), (1, 4))),
        "cotangent": heavy_noise(key_of[13], (NSEQ, SEQ_LEN, MODEL_DIMENSION), 1.0, 6.0, ((0, 4), (1, 4)), (1, 2, 4, 2.0)),
    }


EPS = 1e-06
THETA = 1000000.0
MASKED = -1000000000.0

@jax.custom_vjp
def reduced_precision(v):
    return lax.optimization_barrier(v.astype(jnp.bfloat16)).astype(jnp.float32)

@jax.custom_vjp
def reduced_backward(v):
    return v

def low_keep(v):
    return (reduced_precision(v), None)

def low_pass(kept, grad):
    return (grad,)

def back_keep(v):
    return (v, None)

def back_low(kept, grad):
    return (reduced_precision(grad),)
reduced_precision.defvjp(low_keep, low_pass)
reduced_backward.defvjp(back_keep, back_low)

def precise_product(left, right):
    return jnp.dot(left, right, precision=lax.Precision.HIGHEST, preferred_element_type=jnp.float32)

def rms_factor(values):
    return lax.rsqrt(lax.optimization_barrier(jnp.mean(values * values, axis=-1, keepdims=True)) + EPS)

def doc_positions(segments):
    sequence_length = segments.shape[-1]
    places = jnp.arange(sequence_length, dtype=jnp.int32)
    earlier = jnp.concatenate([segments[:, :1], segments[:, :-1]], axis=1)
    starts = jnp.where(segments != earlier, places[None, :], 0)
    return places[None, :] - lax.cummax(starts, axis=1)

def rotary_tables(positions):
    half_dim = HEAD_SIZE // 2
    frequencies = THETA ** (-(2.0 * jnp.arange(half_dim, dtype=jnp.float32)) / HEAD_SIZE)
    angles = positions.astype(jnp.float32)[..., None] * frequencies
    return (jnp.cos(angles), jnp.sin(angles))

def rotate(values, rot_cos, rot_sin):
    half_dim = values.shape[-1] // 2
    front_half = values[..., :half_dim]
    back_half = values[..., half_dim:]
    cos_part = rot_cos[..., None, :]
    sin_part = rot_sin[..., None, :]
    return jnp.concatenate([front_half * cos_part - back_half * sin_part, back_half * cos_part + front_half * sin_part], axis=-1)

def attend_one(query_rot, rotary_key, value_reduced, seg_row):
    sequence_length = seg_row.shape[0]
    places = jnp.arange(sequence_length, dtype=jnp.int32)
    allowed = (seg_row[:, None] == seg_row[None, :]) & (places[None, :] <= places[:, None])
    key_row_matrix = jnp.repeat(rotary_key, QUERY_HEADS // KEY_VALUE_HEADS, axis=1)
    value_row_matrix = jnp.repeat(value_reduced, QUERY_HEADS // KEY_VALUE_HEADS, axis=1)
    scores = reduced_backward(jnp.einsum('qhd,khd->hqk', query_rot, key_row_matrix, precision=lax.Precision.HIGHEST) / math.sqrt(HEAD_SIZE))
    scores = jnp.where(allowed[None], scores, MASKED)
    row_max = lax.optimization_barrier(jnp.max(scores, axis=-1, keepdims=True))
    weights = jnp.exp(scores - row_max)
    attn_probs = weights / lax.optimization_barrier(jnp.sum(weights, axis=-1, keepdims=True))
    mixed = jnp.einsum('hqk,khd->qhd', reduced_precision(attn_probs), value_row_matrix, precision=lax.Precision.HIGHEST)
    return reduced_precision(reduced_backward(mixed))

def layer(inputs, input_gain, middle_gain, query_gain, key_gain, w_query, key_projection_weight, value_projection_weight, w_out, w_gate, w_up, w_down, rot_cos, rot_sin, seg_block):
    block_share, sequence_length = (inputs.shape[0], inputs.shape[1])
    first_activation = reduced_precision(inputs * rms_factor(inputs) * input_gain)
    query_raw = reduced_backward(precise_product(first_activation, w_query)).reshape(block_share, sequence_length, QUERY_HEADS, HEAD_SIZE)
    unrotated_key = reduced_backward(precise_product(first_activation, key_projection_weight)).reshape(block_share, sequence_length, KEY_VALUE_HEADS, HEAD_SIZE)
    value_reduced = reduced_precision(reduced_backward(precise_product(first_activation, value_projection_weight))).reshape(block_share, sequence_length, KEY_VALUE_HEADS, HEAD_SIZE)
    query_rot = reduced_precision(rotate(query_raw * rms_factor(query_raw) * query_gain, rot_cos, rot_sin))
    rotary_key = reduced_precision(rotate(unrotated_key * rms_factor(unrotated_key) * key_gain, rot_cos, rot_sin))
    mixed = lax.map(lambda element: jax.checkpoint(attend_one)(*element), (query_rot, rotary_key, value_reduced, seg_block))
    mixed = mixed.reshape(block_share, sequence_length, QUERY_HEADS * HEAD_SIZE)
    residual = inputs + reduced_backward(precise_product(mixed, w_out))
    act_two = reduced_precision(residual * rms_factor(residual) * middle_gain)
    gate_value = reduced_backward(precise_product(act_two, w_gate))
    up_value = reduced_backward(precise_product(act_two, w_up))
    hidden = reduced_precision(gate_value * jax.nn.sigmoid(gate_value) * up_value)
    return residual + precise_product(hidden, w_down)

def reference(tokens, segments, input_gain, middle_gain, query_gain, key_gain, w_query, key_projection_weight, value_projection_weight, w_out, w_gate, w_up, w_down, cotangent):
    weights = tuple((weight.astype(jnp.float32) for weight in (input_gain, middle_gain, query_gain, key_gain, w_query, key_projection_weight, value_projection_weight, w_out, w_gate, w_up, w_down)))
    seq_count = tokens.shape[0]
    block_share = math.gcd(seq_count, 4)
    block_count = seq_count // block_share
    positions = doc_positions(segments)
    rot_cos, rot_sin = rotary_tables(positions)

    def blocked(array):
        return array.reshape((block_count, block_share) + array.shape[1:])

    def scan_step(totals, element):
        input_block, cot_block, seg_block, cos_block, sin_block = element

        def forward(inputs, *params):
            return layer(inputs, *params, cos_block, sin_block, seg_block)
        outputs, pullback = jax.vjp(forward, input_block.astype(jnp.float32), *weights)
        gradients = pullback(cot_block.astype(jnp.float32))
        totals = tuple((total + grad for total, grad in zip(totals, gradients[1:])))
        return (totals, (outputs.astype(jnp.bfloat16), gradients[0].astype(jnp.bfloat16)))
    zeros = tuple((jnp.zeros(weight.shape, jnp.float32) for weight in weights))
    totals, (out_blocks, grad_blocks) = lax.scan(scan_step, zeros, (blocked(tokens), blocked(cotangent), blocked(segments), blocked(rot_cos), blocked(rot_sin)))
    return (out_blocks.reshape(tokens.shape), grad_blocks.reshape(tokens.shape), totals[0], totals[1], totals[2], totals[3], totals[4], totals[5], totals[6], totals[7], totals[8], totals[9], totals[10])
```

```python
import math

import jax
import jax.numpy as jnp
from jax import lax
from jax.sharding import PartitionSpec as P

EPS = 1e-06
THETA = 1000000.0
MASKED = -1000000000.0


def rms_factor(values):
    return lax.rsqrt(jnp.mean(values * values, axis=-1, keepdims=True) + EPS)


def rms_backward(grad_out, normed, factor, gain_vec):
    scaled = grad_out * gain_vec
    return factor * (scaled - normed * jnp.mean(scaled * normed, axis=-1, keepdims=True))


def doc_positions(segments):
    sequence_length = segments.shape[-1]
    places = jnp.arange(sequence_length, dtype=jnp.int32)
    lower = segments[:, None, :] < segments[:, :, None]
    return places[None, :] - jnp.sum(lower.astype(jnp.int32), axis=-1)


def rotary_tables(positions, head_dim):
    half_dim = head_dim // 2
    frequencies = THETA ** (-(2.0 * jnp.arange(half_dim, dtype=jnp.float32)) / head_dim)
    angles = positions.astype(jnp.float32)[..., None] * frequencies
    return (jnp.cos(angles), jnp.sin(angles))


def rotate(values, rot_cos, rot_sin, direction):
    half_dim = values.shape[-1] // 2
    front_half = values[..., :half_dim]
    back_half = values[..., half_dim:]
    return jnp.concatenate(
        [
            front_half * rot_cos - direction * back_half * rot_sin,
            back_half * rot_cos + direction * front_half * rot_sin,
        ],
        axis=-1,
    )


def block_group(seq_count, local_len):
    block_share = 1
    for candidate in range(1, seq_count + 1):
        if seq_count % candidate == 0 and candidate * local_len <= 512:
            block_share = candidate
    return block_share


def local(
    tokens,
    segments,
    input_gain,
    middle_gain,
    query_gain,
    key_gain,
    w_query,
    key_projection_weight,
    value_projection_weight,
    w_out,
    w_gate,
    w_up,
    w_down,
    cotangent,
):
    (
        input_gain,
        middle_gain,
        query_gain,
        key_gain,
        w_query,
        key_projection_weight,
        value_projection_weight,
        w_out,
        w_gate,
        w_up,
        w_down,
    ) = (
        lax.all_gather(input_gain, "fsdp", axis=0, tiled=True),
        lax.all_gather(middle_gain, "fsdp", axis=0, tiled=True),
        lax.all_gather(query_gain, "fsdp", axis=0, tiled=True),
        lax.all_gather(key_gain, "fsdp", axis=0, tiled=True),
        lax.all_gather(w_query, "fsdp", axis=0, tiled=True),
        lax.all_gather(key_projection_weight, "fsdp", axis=0, tiled=True),
        lax.all_gather(value_projection_weight, "fsdp", axis=0, tiled=True),
        lax.all_gather(w_out, "fsdp", axis=1, tiled=True),
        lax.all_gather(w_gate, "fsdp", axis=0, tiled=True),
        lax.all_gather(w_up, "fsdp", axis=0, tiled=True),
        lax.all_gather(w_down, "fsdp", axis=1, tiled=True),
    )
    seq_count, local_len, model_width = tokens.shape
    sequence_length = segments.shape[1]
    head_dim = query_gain.shape[0]
    q_heads = w_query.shape[1] // head_dim
    kv_heads = key_projection_weight.shape[1] // head_dim
    head_repeats = q_heads // kv_heads
    row_count = seq_count * local_len
    block_share = block_group(seq_count, local_len)
    block_count = seq_count // block_share
    contract_last = (((1,), (1,)), ((), ()))
    contract_first = (((0,), (0,)), ((), ()))
    inv_root = 1.0 / math.sqrt(head_dim)
    row_offset = lax.axis_index("context") * local_len
    positions = doc_positions(segments)
    local_pos = lax.dynamic_slice_in_dim(positions, row_offset, local_len, 1)
    query_segs = lax.dynamic_slice_in_dim(segments, row_offset, local_len, 1)
    rot_cos, rot_sin = rotary_tables(local_pos, head_dim)
    rot_cos = rot_cos.reshape(row_count, 1, head_dim // 2)
    rot_sin = rot_sin.reshape(row_count, 1, head_dim // 2)
    query_idx = row_offset + jnp.arange(local_len, dtype=jnp.int32)
    key_idx = jnp.arange(sequence_length, dtype=jnp.int32)
    causal = key_idx[None, :] <= query_idx[:, None]
    inputs = tokens.reshape(row_count, model_width).astype(jnp.float32)
    in_factor = rms_factor(inputs)
    in_normed = inputs * in_factor
    first_activation = (in_normed * input_gain.astype(jnp.float32)).astype(jnp.bfloat16)
    query_raw = jnp.dot(first_activation, w_query, preferred_element_type=jnp.float32).reshape(
        row_count, q_heads, head_dim
    )
    unrotated_key = jnp.dot(
        first_activation, key_projection_weight, preferred_element_type=jnp.float32
    ).reshape(row_count, kv_heads, head_dim)
    value_reduced = jnp.dot(
        first_activation, value_projection_weight, preferred_element_type=jnp.float32
    ).astype(jnp.bfloat16)
    query_factor = rms_factor(query_raw)
    query_normed = query_raw * query_factor
    query_rot = rotate(query_normed * query_gain.astype(jnp.float32), rot_cos, rot_sin, 1.0).astype(
        jnp.bfloat16
    )
    key_factor = rms_factor(unrotated_key)
    key_normed = unrotated_key * key_factor
    rotary_key = rotate(key_normed * key_gain.astype(jnp.float32), rot_cos, rot_sin, 1.0).astype(
        jnp.bfloat16
    )
    key_view = rotary_key.reshape(seq_count, local_len, kv_heads * head_dim)
    value_view = value_reduced.reshape(seq_count, local_len, kv_heads * head_dim)
    keys_all, values_all = (
        lax.all_gather(key_view, "context", axis=1, tiled=True),
        lax.all_gather(value_view, "context", axis=1, tiled=True),
    )

    def blocked(array):
        return array.reshape((block_count, block_share) + array.shape[1:])

    query_blocks = query_rot.reshape(
        block_count, block_share, local_len, kv_heads, head_repeats, head_dim
    )
    qseg_blocks = blocked(query_segs)
    kseg_blocks = blocked(segments)

    def scores_of(query_part, key_row_matrix, qseg, kseg):
        raw_scores = (
            jnp.einsum(
                "gqkrd,gjkd->gkrqj", query_part, key_row_matrix, preferred_element_type=jnp.float32
            )
            * inv_root
        )
        allowed = (qseg[:, :, None] == kseg[:, None, :]) & causal[None]
        return jnp.where(allowed[:, None, None], raw_scores, MASKED)

    def attend_forward(block_parts):
        query_part, key_part, value_part, qseg, kseg = block_parts
        key_row_matrix = key_part.reshape(block_share, sequence_length, kv_heads, head_dim)
        value_row_matrix = value_part.reshape(block_share, sequence_length, kv_heads, head_dim)
        scores = scores_of(query_part, key_row_matrix, qseg, kseg)
        row_max = jnp.max(scores, axis=-1, keepdims=True)
        weights = jnp.exp(scores - row_max)
        row_total = jnp.sum(weights, axis=-1, keepdims=True)
        attn_probs = (weights / row_total).astype(jnp.bfloat16)
        mixed = jnp.einsum(
            "gkrqj,gjkd->gqkrd", attn_probs, value_row_matrix, preferred_element_type=jnp.float32
        )
        return (mixed.astype(jnp.bfloat16), row_max + jnp.log(row_total))

    mixed, log_total = lax.map(
        attend_forward,
        (query_blocks, blocked(keys_all), blocked(values_all), qseg_blocks, kseg_blocks),
    )
    mixed_flat = mixed.reshape(row_count, q_heads * head_dim)
    attn_part = jnp.dot(mixed_flat, w_out, preferred_element_type=jnp.float32)
    middle_f32 = middle_gain.astype(jnp.float32)
    residual = inputs + lax.psum(attn_part, "tensor")
    mid_factor = rms_factor(residual)
    mid_normed = residual * mid_factor
    act_two = (mid_normed * middle_f32).astype(jnp.bfloat16)
    gate_value = jnp.dot(act_two, w_gate, preferred_element_type=jnp.float32)
    up_value = jnp.dot(act_two, w_up, preferred_element_type=jnp.float32)
    sigmoid_gate = jax.nn.sigmoid(gate_value)
    silu_gate = gate_value * sigmoid_gate
    hidden = (silu_gate * up_value).astype(jnp.bfloat16)
    down_part = jnp.dot(hidden, w_down, preferred_element_type=jnp.float32)
    out_low = (
        residual + lax.psum(down_part.astype(jnp.bfloat16), "tensor").astype(jnp.float32)
    ).astype(jnp.bfloat16)
    grad_low = cotangent.reshape(row_count, model_width)
    d_hidden = lax.dot_general(grad_low, w_down, contract_last, preferred_element_type=jnp.float32)
    g_down = lax.dot_general(hidden, grad_low, contract_first, preferred_element_type=jnp.float32)
    d_gate = (
        d_hidden * up_value * sigmoid_gate * (1.0 + gate_value * (1.0 - sigmoid_gate))
    ).astype(jnp.bfloat16)
    d_up = (d_hidden * silu_gate).astype(jnp.bfloat16)
    g_gate = lax.dot_general(act_two, d_gate, contract_first, preferred_element_type=jnp.float32)
    g_up = lax.dot_general(act_two, d_up, contract_first, preferred_element_type=jnp.float32)
    d_act_part = lax.dot_general(d_gate, w_gate, contract_last, preferred_element_type=jnp.float32)
    d_act_part = d_act_part + lax.dot_general(
        d_up, w_up, contract_last, preferred_element_type=jnp.float32
    )
    d_act_two = lax.psum(d_act_part.astype(jnp.bfloat16), "tensor").astype(jnp.float32)
    g_middle = jnp.sum(d_act_two * mid_normed, axis=0)
    d_residual = grad_low.astype(jnp.float32) + rms_backward(
        d_act_two, mid_normed, mid_factor, middle_f32
    )
    d_res_rows = d_residual.astype(jnp.bfloat16)
    block_out = out_low.reshape(seq_count, local_len, model_width)
    g_out = lax.dot_general(
        mixed_flat, d_res_rows, contract_first, preferred_element_type=jnp.float32
    )
    d_mixed = lax.dot_general(
        d_res_rows, w_out, contract_last, preferred_element_type=jnp.float32
    ).astype(jnp.bfloat16)
    keys_back, values_back = (keys_all, values_all)

    def attend_backward(block_parts):
        query_part, key_part, value_part, qseg, kseg, block_lse, d_part = block_parts
        key_row_matrix = key_part.reshape(block_share, sequence_length, kv_heads, head_dim)
        value_row_matrix = value_part.reshape(block_share, sequence_length, kv_heads, head_dim)
        scores = scores_of(query_part, key_row_matrix, qseg, kseg)
        attn_probs = jnp.exp(scores - block_lse)
        d_probs = jnp.einsum(
            "gqkrd,gjkd->gkrqj", d_part, value_row_matrix, preferred_element_type=jnp.float32
        )
        inner_sum = jnp.sum(attn_probs * d_probs, axis=-1, keepdims=True)
        d_scores = (attn_probs * (d_probs - inner_sum)).astype(jnp.bfloat16)
        d_query = (
            jnp.einsum(
                "gkrqj,gjkd->gqkrd", d_scores, key_row_matrix, preferred_element_type=jnp.float32
            )
            * inv_root
        )
        d_keys = (
            jnp.einsum(
                "gkrqj,gqkrd->gjkd", d_scores, query_part, preferred_element_type=jnp.float32
            )
            * inv_root
        )
        d_values = jnp.einsum(
            "gkrqj,gqkrd->gjkd",
            attn_probs.astype(jnp.bfloat16),
            d_part,
            preferred_element_type=jnp.float32,
        )
        return (
            d_query,
            d_keys.reshape(block_share, sequence_length, kv_heads * head_dim),
            d_values.reshape(block_share, sequence_length, kv_heads * head_dim),
        )

    d_mixed_blocks = d_mixed.reshape(
        block_count, block_share, local_len, kv_heads, head_repeats, head_dim
    )
    d_query, d_keys_full, d_values_full = lax.map(
        attend_backward,
        (
            query_blocks,
            blocked(keys_back),
            blocked(values_back),
            qseg_blocks,
            kseg_blocks,
            log_total,
            d_mixed_blocks,
        ),
    )
    d_keys_full = d_keys_full.reshape(seq_count, sequence_length, kv_heads * head_dim)
    d_values_full = d_values_full.reshape(seq_count, sequence_length, kv_heads * head_dim)
    d_keys, d_values = (
        lax.psum_scatter(
            d_keys_full.astype(jnp.bfloat16), "context", scatter_dimension=1, tiled=True
        ).astype(jnp.float32),
        lax.psum_scatter(
            d_values_full.astype(jnp.bfloat16), "context", scatter_dimension=1, tiled=True
        ).astype(jnp.float32),
    )
    d_query_rot = rotate(d_query.reshape(row_count, q_heads, head_dim), rot_cos, rot_sin, -1.0)
    g_query_gain = jnp.sum(d_query_rot * query_normed, axis=(0, 1))
    d_query_raw = rms_backward(
        d_query_rot, query_normed, query_factor, query_gain.astype(jnp.float32)
    )
    d_query_raw = d_query_raw.astype(jnp.bfloat16).reshape(row_count, q_heads * head_dim)
    d_key_rot = rotate(d_keys.reshape(row_count, kv_heads, head_dim), rot_cos, rot_sin, -1.0)
    g_key_gain = jnp.sum(d_key_rot * key_normed, axis=(0, 1))
    d_key_raw = rms_backward(d_key_rot, key_normed, key_factor, key_gain.astype(jnp.float32))
    d_key_raw = d_key_raw.astype(jnp.bfloat16).reshape(row_count, kv_heads * head_dim)
    d_value_low = d_values.reshape(row_count, kv_heads * head_dim).astype(jnp.bfloat16)
    g_query = lax.dot_general(
        first_activation, d_query_raw, contract_first, preferred_element_type=jnp.float32
    )
    g_key = lax.dot_general(
        first_activation, d_key_raw, contract_first, preferred_element_type=jnp.float32
    )
    g_value = lax.dot_general(
        first_activation, d_value_low, contract_first, preferred_element_type=jnp.float32
    )
    d_first = lax.dot_general(
        d_query_raw, w_query, contract_last, preferred_element_type=jnp.float32
    )
    d_first = d_first + lax.dot_general(
        d_key_raw, key_projection_weight, contract_last, preferred_element_type=jnp.float32
    )
    d_first = d_first + lax.dot_general(
        d_value_low, value_projection_weight, contract_last, preferred_element_type=jnp.float32
    )
    input_f32 = input_gain.astype(jnp.float32)
    d_act_one, g_query_gain, g_key_gain = (
        lax.psum(d_first.astype(jnp.bfloat16), "tensor").astype(jnp.float32),
        lax.psum(g_query_gain.astype(jnp.bfloat16), "tensor").astype(jnp.float32),
        lax.psum(g_key_gain.astype(jnp.bfloat16), "tensor").astype(jnp.float32),
    )
    g_input = jnp.sum(d_act_one * in_normed, axis=0)
    d_inputs = d_residual + rms_backward(d_act_one, in_normed, in_factor, input_f32)
    grad_flat = d_inputs.astype(jnp.bfloat16)
    grad_tokens = grad_flat.reshape(seq_count, local_len, model_width)
    (
        g_input,
        g_middle,
        g_query_gain,
        g_key_gain,
        g_query,
        g_key,
        g_value,
        g_out,
        g_gate,
        g_up,
        g_down,
    ) = (
        lax.psum_scatter(
            g_input.astype(jnp.bfloat16), "fsdp", scatter_dimension=0, tiled=True
        ).astype(jnp.float32),
        lax.psum_scatter(
            g_middle.astype(jnp.bfloat16), "fsdp", scatter_dimension=0, tiled=True
        ).astype(jnp.float32),
        lax.psum_scatter(
            g_query_gain.astype(jnp.bfloat16), "fsdp", scatter_dimension=0, tiled=True
        ).astype(jnp.float32),
        lax.psum_scatter(
            g_key_gain.astype(jnp.bfloat16), "fsdp", scatter_dimension=0, tiled=True
        ).astype(jnp.float32),
        lax.psum_scatter(
            g_query.astype(jnp.bfloat16), "fsdp", scatter_dimension=0, tiled=True
        ).astype(jnp.float32),
        lax.psum_scatter(
            g_key.astype(jnp.bfloat16), "fsdp", scatter_dimension=0, tiled=True
        ).astype(jnp.float32),
        lax.psum_scatter(
            g_value.astype(jnp.bfloat16), "fsdp", scatter_dimension=0, tiled=True
        ).astype(jnp.float32),
        lax.psum_scatter(
            g_out.astype(jnp.bfloat16), "fsdp", scatter_dimension=1, tiled=True
        ).astype(jnp.float32),
        lax.psum_scatter(
            g_gate.astype(jnp.bfloat16), "fsdp", scatter_dimension=0, tiled=True
        ).astype(jnp.float32),
        lax.psum_scatter(g_up.astype(jnp.bfloat16), "fsdp", scatter_dimension=0, tiled=True).astype(
            jnp.float32
        ),
        lax.psum_scatter(
            g_down.astype(jnp.bfloat16), "fsdp", scatter_dimension=1, tiled=True
        ).astype(jnp.float32),
    )
    (
        g_input,
        g_middle,
        g_query_gain,
        g_key_gain,
        g_query,
        g_key,
        g_value,
        g_out,
        g_gate,
        g_up,
        g_down,
    ) = (
        lax.psum(g_input.astype(jnp.bfloat16), "context").astype(jnp.float32),
        lax.psum(g_middle.astype(jnp.bfloat16), "context").astype(jnp.float32),
        lax.psum(g_query_gain.astype(jnp.bfloat16), "context").astype(jnp.float32),
        lax.psum(g_key_gain.astype(jnp.bfloat16), "context").astype(jnp.float32),
        lax.psum(g_query.astype(jnp.bfloat16), "context").astype(jnp.float32),
        lax.psum(g_key.astype(jnp.bfloat16), "context").astype(jnp.float32),
        lax.psum(g_value.astype(jnp.bfloat16), "context").astype(jnp.float32),
        lax.psum(g_out.astype(jnp.bfloat16), "context").astype(jnp.float32),
        lax.psum(g_gate.astype(jnp.bfloat16), "context").astype(jnp.float32),
        lax.psum(g_up.astype(jnp.bfloat16), "context").astype(jnp.float32),
        lax.psum(g_down.astype(jnp.bfloat16), "context").astype(jnp.float32),
    )
    return (
        block_out,
        grad_tokens,
        g_input,
        g_middle,
        g_query_gain,
        g_key_gain,
        g_query,
        g_key,
        g_value,
        g_out,
        g_gate,
        g_up,
        g_down,
    )


def solution(mesh):
    return jax.shard_map(
        local,
        mesh=mesh,
        in_specs=(
            P("fsdp", "context", None),
            P("fsdp", None),
            P("fsdp"),
            P("fsdp"),
            P("fsdp"),
            P("fsdp"),
            P("fsdp", "tensor"),
            P("fsdp", "tensor"),
            P("fsdp", "tensor"),
            P("tensor", "fsdp"),
            P("fsdp", "tensor"),
            P("fsdp", "tensor"),
            P("tensor", "fsdp"),
            P("fsdp", "context", None),
        ),
        out_specs=(
            P("fsdp", "context", None),
            P("fsdp", "context", None),
            P("fsdp"),
            P("fsdp"),
            P("fsdp"),
            P("fsdp"),
            P("fsdp", "tensor"),
            P("fsdp", "tensor"),
            P("fsdp", "tensor"),
            P("tensor", "fsdp"),
            P("fsdp", "tensor"),
            P("fsdp", "tensor"),
            P("tensor", "fsdp"),
        ),
        check_vma=False,
    )
```
